128 devices in a mesh: rep: 16 (over z, y), shard: 8 (over x, core).
Axes of the slice: x: 4, y: 4, z: 4, core: 2. Of those that a mesh axis runs over, the one named last changes fastest.
Arguments:
- grads: bfloat16 [16, 8, 1024, 1024], P('rep', 'shard'), may hold values from -6 to 6
- master: float32 [8, 256, 1024], P('shard'), may hold values from -4 to 4
- moment_one: float32 [8, 256, 1024], P('shard'), may hold values from -4 to 4
- moment_two: float32 [8, 256, 1024], P('shard'), may hold values from 0.01 to 10
- average: float32 [8, 256, 1024], P('shard'), may hold values from -4 to 4
- tensor_owner: int32 [32], replicated, may hold values from 0 to 7, as said below
- tensor_start: int32 [32], replicated, may hold values from 0 to 1008, as said below
- tensor_rows: int32 [32], replicated, may hold values from 16 to 208, as said below
- tensor_slot: int32 [32], replicated, may hold values from 0 to 240, as said below
Outputs:
- new_params: float32 [1024, 1024], replicated
- master_new: float32 [8, 256, 1024], P('shard')
- moment_one_new: float32 [8, 256, 1024], P('shard')
- moment_two_new: float32 [8, 256, 1024], P('shard')
- average_new: float32 [8, 256, 1024], P('shard')
The draws below stay inside these ranges and needn't reach their ends.
Inputs may be any that keep to these rules, and one draw needn't show every extreme that they name: `tensor_owner`: every owner holds exactly 4 tensors; one owner's tensors have exactly 256 rows together and no owner's more. `tensor_start`: the tensors cover the window's rows without gaps or intersections. `tensor_rows`: each tensor's rows are a multiple of 16. `tensor_slot`: an owner's tensors fill its buffer rows from 0 upward without gaps or intersections.
All inputs are finite; a program needn't handle non-finite values.
Results may differ from the reference program's by a relative error of at most 0.0003.
Values may be sent and summed in bfloat16 or wider, within the bound.
No kernel may reach another device: no remote copies, remote signals or barrier semaphores. Data moves between devices by JAX's collectives and lax.ppermute only.
A program may use at most 128 MiB of HBM per device.

```python
import math
import jax
import jax.numpy as jnp
from jax import lax

WIDTH = 1024
OWN_ROWS = 128
UNIT = 16
TEN_OWN = 4
REPLICAS = 16
OWNERS = 8
ROWS = 1024
CAP = 256
TENSORS = 32
N_REP = 16
N_SHARD = 8


def ownership(key):
    unit_count = OWN_ROWS // UNIT
    subkeys = jax.random.split(jax.random.fold_in(key, 11), 4)
    busiest = jax.random.randint(subkeys[0], (), 0, N_SHARD, dtype=jnp.int32)
    others = N_SHARD - 1
    remaining = (N_SHARD - 2) * unit_count
    base_load = remaining // others
    leftover = remaining - others * base_load
    jitter_range = base_load // 4
    jitter = jax.random.randint(subkeys[1], (others,), -jitter_range, jitter_range + 1, dtype=jnp.int32)
    position = jnp.arange(others, dtype=jnp.int32)
    paired = jnp.where(position % 2 == 0, jitter, -jnp.roll(jitter, 1))
    paired = jnp.where(position == others - 1, leftover, paired)
    owner_of = (busiest + 1 + position) % N_SHARD
    owner_loads = jnp.zeros((N_SHARD,), jnp.int32).at[owner_of].set(base_load + paired)
    owner_loads = owner_loads.at[busiest].set(2 * unit_count)
    weights = jax.random.randint(subkeys[2], (N_SHARD, TEN_OWN), 1, 5, dtype=jnp.int32)
    spare_units = owner_loads - TEN_OWN
    unit_parts = 1 + weights * spare_units[:, None] // jnp.sum(weights, axis=1, keepdims=True)
    unit_parts = unit_parts.at[:, TEN_OWN - 1].add(owner_loads - jnp.sum(unit_parts, axis=1))
    column = jnp.arange(TEN_OWN, dtype=jnp.int32)
    busiest_parts = jnp.where(column == 0, 2 * unit_count - (TEN_OWN - 1), 1).astype(jnp.int32)
    unit_parts = unit_parts.at[busiest].set(busiest_parts)
    part_rows = unit_parts * UNIT
    part_slots = jnp.cumsum(part_rows, axis=1) - part_rows
    last_index = (busiest * TEN_OWN + TEN_OWN - 1).astype(jnp.int32)
    rest = jax.random.permutation(subkeys[3], TENSORS - 1).astype(jnp.int32)
    rest = rest + (rest >= last_index).astype(jnp.int32)
    placing = jnp.concatenate([rest, last_index[None]]).astype(jnp.int32)
    owner_flat = jnp.repeat(jnp.arange(N_SHARD, dtype=jnp.int32), TEN_OWN, total_repeat_length=TENSORS)
    rows_placed = part_rows.reshape(TENSORS)[placing].astype(jnp.int32)
    tensor_starts = (jnp.cumsum(rows_placed) - rows_placed).astype(jnp.int32)
    return (owner_flat[placing], tensor_starts, rows_placed, part_slots.reshape(TENSORS)[placing].astype(jnp.int32))


def draw_tensor_owner(key, part):
    return ownership(key)[0]


def draw_tensor_start(key, part):
    return ownership(key)[1]


def draw_tensor_rows(key, part):
    return ownership(key)[2]


def draw_tensor_slot(key, part):
    return ownership(key)[3]


def block_scale(own_key, extent, pieces, smallest, high):
    loudness, own = 1.0, jax.random.fold_in(own_key, 6)
    for axis_at, parts in pieces:
        steps = jnp.exp(jax.random.uniform(jax.random.fold_in(own, axis_at), (parts,), jnp.float32, smallest / len(pieces), high / len(pieces)))
        loudness = loudness * jnp.repeat(steps, extent[axis_at] // parts).reshape([-1 if axis == axis_at else 1 for axis in range(len(extent))])
    return loudness


def bell_draw(stream_key, shape, width, most, pieces=(), held_as=jnp.bfloat16):
    gain = block_scale(stream_key, shape, pieces, -0.22, 0.18) if pieces else 1.0
    drawn = jax.random.normal(stream_key, shape, jnp.float32) * width * gain
    return jnp.minimum(jnp.maximum(drawn, -most), most).astype(held_as)


def setup_inputs(seed: int = 0) -> dict:
    key_list = jax.random.split(jax.random.key(seed), 10)
    return {
        "grads": bell_draw(key_list[0], (REPLICAS, OWNERS, ROWS, WIDTH), 1.0, 6.0, ((0, 16), (1, 8))),
        "master": bell_draw(key_list[1], (OWNERS, CAP, WIDTH), 0.5, 4.0, ((0, 8),), jnp.float32),
        "moment_one": bell_draw(key_list[2], (OWNERS, CAP, WIDTH), 0.5, 4.0, ((0, 8),), jnp.float32),
        "moment_two": jnp.clip(jnp.exp(math.log(10.0) - 6.9077553 * jax.random.uniform(key_list[3], (OWNERS, CAP, WIDTH), jnp.float32) ** block_scale(key_list[3], (OWNERS, CAP, WIDTH), ((0, 8),), -0.2, 0.2)), 0.01, 10.0),
        "average": bell_draw(key_list[4], (OWNERS, CAP, WIDTH), 0.5, 4.0, ((0, 8),), jnp.float32),
        "tensor_owner": draw_tensor_owner(jax.random.fold_in(key_list[9], 71), 0),
        "tensor_start": draw_tensor_start(jax.random.fold_in(key_list[9], 71), 0),
        "tensor_rows": draw_tensor_rows(jax.random.fold_in(key_list[9], 71), 0),
        "tensor_slot": draw_tensor_slot(jax.random.fold_in(key_list[9], 71), 0),
    }


beta_one = 0.9
beta_two = 0.95
epsilon = 1e-08
learn_rate = 0.01
decay_base = 0.1
average_rate = 0.99
step_count = 10.0
reference_batch = 128.0

def optimizer_step(summed, master, moment_one, moment_two, average, decay_scale):
    moment_one_new = beta_one * moment_one + (1.0 - beta_one) * summed
    moment_two_new = beta_two * moment_two + (1.0 - beta_two) * summed * summed
    corr_one = 1.0 - beta_one ** step_count
    corr_two = 1.0 - beta_two ** step_count
    update = moment_one_new / corr_one / (jnp.sqrt(moment_two_new / corr_two) + epsilon)
    master_new = master * (1.0 - learn_rate * decay_base * decay_scale) - learn_rate * update
    average_new = average_rate * average + (1.0 - average_rate) * master_new
    return (master_new, moment_one_new, moment_two_new, average_new)

def reference(grads, master, moment_one, moment_two, average, tensor_owner, tensor_start, tensor_rows, tensor_slot):
    row_index = jnp.arange(ROWS, dtype=jnp.int32)
    inside = (row_index[:, None] >= tensor_start[None, :]) & (row_index[:, None] < (tensor_start + tensor_rows)[None, :])
    target = (tensor_owner * CAP + tensor_slot - tensor_start).astype(jnp.int32)
    destination = lax.optimization_barrier(jnp.sum(jnp.where(inside, target[None, :] + row_index[:, None], 0), axis=1)).astype(jnp.int32)
    summed_rows = lax.optimization_barrier(jnp.sum(grads, axis=(0, 1), dtype=jnp.float32))
    summed = jnp.zeros((N_SHARD * CAP, WIDTH), jnp.float32).at[destination].set(summed_rows)
    summed = summed.reshape(N_SHARD, CAP, WIDTH)
    decay_scale = math.sqrt(N_REP * N_SHARD / reference_batch)
    master_new, moment_one_new, moment_two_new, average_new = optimizer_step(summed, master, moment_one, moment_two, average, decay_scale)
    new_params = master_new.reshape(N_SHARD * CAP, WIDTH)[destination]
    return (new_params, master_new, moment_one_new, moment_two_new, average_new)
```

```python
import math

import jax
import jax.numpy as jnp
from jax import lax
from jax.experimental import pallas as pl
from jax.experimental.pallas import tpu as pltpu
from jax.sharding import Mesh, PartitionSpec as P

beta_one = 0.9
beta_two = 0.95
epsilon = 1e-08
learn_rate = 0.01
decay_base = 0.1
average_rate = 0.99
step_count = 10.0
reference_batch = 128.0

REP = ("z", "y")
SHARD = ("x", "core")
ALL = REP + SHARD
N_REP, N_SHARD = 16, 8
UNIT, SUB, LANES = 16, 8, 128
decay_scale = math.sqrt(N_REP * N_SHARD / reference_batch)


def new_master(summed, master, moment_one, moment_two):
    moment_one_new = beta_one * moment_one + (1.0 - beta_one) * summed
    moment_two_new = beta_two * moment_two + (1.0 - beta_two) * summed * summed
    corr_one = 1.0 - beta_one**step_count
    corr_two = 1.0 - beta_two**step_count
    update = moment_one_new / corr_one / (jnp.sqrt(moment_two_new / corr_two) + epsilon)
    master_new = master * (1.0 - learn_rate * decay_base * decay_scale) - learn_rate * update
    return master_new, moment_one_new, moment_two_new


def state_kernel(tiles, master, one, two, average, master_out, one_out, two_out, average_out):
    for unit in range(tiles.shape[1]):
        for half in range(2):
            rows = pl.ds(unit * UNIT + half * SUB, SUB)
            for block in range(N_REP // 2):
                cols = pl.ds(block * LANES, LANES)
                summed = tiles[block * 2 + half, unit]
                m, a, b = new_master(summed, master[rows, cols], one[rows, cols], two[rows, cols])
                master_out[rows, cols] = m
                one_out[rows, cols] = a
                two_out[rows, cols] = b
                average_out[rows, cols] = (
                    average_rate * average[rows, cols] + (1.0 - average_rate) * m
                )


def owner_update(tiles, master, one, two, average):
    rows, width = master.shape
    units = 2
    steps = rows // (units * UNIT)
    block = pl.BlockSpec((units * UNIT, width), lambda s: (s, 0))
    return pl.pallas_call(
        state_kernel,
        grid=(steps,),
        in_specs=[pl.BlockSpec((N_REP, units, SUB, LANES), lambda s: (0, s, 0, 0))] + [block] * 4,
        out_specs=[block] * 4,
        out_shape=[jax.ShapeDtypeStruct((rows, width), jnp.float32)] * 4,
        cost_estimate=pl.CostEstimate(
            flops=20 * rows * width, bytes_accessed=36 * rows * width, transcendentals=rows * width
        ),
        name="owner_update",
    )(tiles, master, one, two, average)


def local(
    grads,
    master,
    moment_one,
    moment_two,
    average,
    tensor_owner,
    tensor_start,
    tensor_rows,
    tensor_slot,
):
    gradient = grads[0, 0]
    row_total, width = gradient.shape
    capacity = master.shape[1]
    blocks = width // LANES
    units = row_total // UNIT
    own_units = units // N_SHARD
    slots = capacity // UNIT
    rep = lax.axis_index(REP)
    shard = lax.axis_index(SHARD)
    col, half = rep // 2, rep % 2

    first = jnp.arange(units, dtype=jnp.int32) * UNIT
    inside = (first[:, None] >= tensor_start[None, :]) & (
        first[:, None] < (tensor_start + tensor_rows)[None, :]
    )
    home = tensor_owner * capacity + tensor_slot - tensor_start
    unit_home = jnp.sum(jnp.where(inside, home[None, :] + first[:, None], 0), axis=1) // UNIT
    slot_first = jnp.arange(slots, dtype=jnp.int32) * UNIT
    held = (
        (tensor_owner[None, :] == shard)
        & (slot_first[:, None] >= tensor_slot[None, :])
        & (slot_first[:, None] < (tensor_slot + tensor_rows)[None, :])
    )
    source = tensor_start - tensor_slot
    slot_unit = jnp.sum(jnp.where(held, source[None, :] + slot_first[:, None], 0), axis=1) // UNIT
    slot_used = jnp.any(held, axis=1)

    def my_tiles(state):
        state = state.reshape(slots, 2, SUB, blocks, LANES)
        return lax.dynamic_slice(
            state, (0, half, 0, col, 0), (slots, 1, SUB, 1, LANES)
        ).reshape(slots, SUB, LANES)

    mine = jnp.stack([my_tiles(s[0]) for s in (master, moment_one, moment_two)], axis=1)
    states = lax.all_gather(mine, SHARD, axis=0, tiled=True)

    packed = gradient.reshape(N_SHARD, own_units, 2, SUB, blocks, LANES)
    packed = packed.transpose(4, 2, 0, 1, 3, 5).reshape(N_REP * N_SHARD, own_units, SUB, LANES)
    received = lax.all_to_all(packed, ALL, split_axis=0, concat_axis=0, tiled=True)
    summed = jnp.sum(received, axis=0, dtype=jnp.float32)

    my_home = lax.dynamic_slice(unit_home, (shard * own_units,), (own_units,))
    picked = jnp.take(states, my_home, axis=0)
    weights, _, _ = new_master(summed, picked[:, 0], picked[:, 1], picked[:, 2])

    spread = jnp.broadcast_to(weights, (N_REP, *weights.shape))
    spread = lax.all_to_all(spread, REP, split_axis=0, concat_axis=0, tiled=True)
    lines = spread.reshape(blocks, 2, own_units, SUB, LANES).transpose(2, 1, 3, 0, 4)
    lines = lines.reshape(own_units * UNIT, width)
    new_params = lax.all_gather(lines, SHARD, axis=0, tiled=True)

    summed, _ = lax.optimization_barrier((summed, lines))
    window = jnp.broadcast_to(summed, (N_SHARD, *summed.shape))
    window = lax.all_to_all(window, SHARD, split_axis=0, concat_axis=0, tiled=True)
    window = window.reshape(units, SUB, LANES)
    own = jnp.take(window, slot_unit, axis=0)
    own = jnp.where(slot_used[:, None, None], own, 0.0)
    tiles = jnp.broadcast_to(own, (N_REP, *own.shape))
    tiles = lax.all_to_all(tiles, REP, split_axis=0, concat_axis=0, tiled=True)
    outs = owner_update(tiles, master[0], moment_one[0], moment_two[0], average[0])
    return (new_params, *(o[None] for o in outs))


def solution(mesh):
    grid = Mesh(mesh.devices.reshape(4, 4, 4, 2), ALL)
    state = P(SHARD, None, None)
    in_specs = (P(REP, SHARD, None, None), state, state, state, state, P(), P(), P(), P())
    out_specs = (P(), state, state, state, state)
    return jax.shard_map(local, mesh=grid, in_specs=in_specs, out_specs=out_specs, check_vma=False)
```

```python
import math

import jax
import jax.numpy as jnp
from jax import lax
from jax.experimental import pallas as pl
from jax.experimental.pallas import tpu as pltpu
from jax.sharding import Mesh, PartitionSpec as P

beta_one = 0.9
beta_two = 0.95
epsilon = 1e-08
learn_rate = 0.01
decay_base = 0.1
average_rate = 0.99
step_count = 10.0
reference_batch = 128.0

REP = ("z", "y")
SHARD = ("x", "core")
ALL = REP + SHARD
N_REP, N_SHARD = 16, 8
UNIT, SUB, LANES = 16, 8, 128
decay_scale = math.sqrt(N_REP * N_SHARD / reference_batch)


def new_master(summed, master, moment_one, moment_two):
    moment_one_new = beta_one * moment_one + (1.0 - beta_one) * summed
    moment_two_new = beta_two * moment_two + (1.0 - beta_two) * summed * summed
    moment = moment_one_new * (1.0 / (1.0 - beta_one**step_count))
    spread = jnp.sqrt(moment_two_new * (1.0 / (1.0 - beta_two**step_count)))
    update = moment / (spread + epsilon)
    master_new = master * (1.0 - learn_rate * decay_base * decay_scale) - learn_rate * update
    return master_new, moment_one_new, moment_two_new


def state_kernel(tiles, master, one, two, average, master_out, one_out, two_out, average_out):
    for unit in range(tiles.shape[1]):
        for half in range(2):
            rows = pl.ds(unit * UNIT + half * SUB, SUB)
            for block in range(N_REP // 2):
                cols = pl.ds(block * LANES, LANES)
                summed = tiles[block * 2 + half, unit]
                m, a, b = new_master(summed, master[rows, cols], one[rows, cols], two[rows, cols])
                master_out[rows, cols] = m
                one_out[rows, cols] = a
                two_out[rows, cols] = b
                average_out[rows, cols] = (
                    average_rate * average[rows, cols] + (1.0 - average_rate) * m
                )


def owner_update(tiles, master, one, two, average):
    rows, width = master.shape
    units = 2
    steps = rows // (units * UNIT)
    block = pl.BlockSpec((units * UNIT, width), lambda s: (s, 0))
    return pl.pallas_call(
        state_kernel,
        grid=(steps,),
        in_specs=[pl.BlockSpec((N_REP, units, SUB, LANES), lambda s: (0, s, 0, 0))] + [block] * 4,
        out_specs=[block] * 4,
        out_shape=[jax.ShapeDtypeStruct((rows, width), jnp.float32)] * 4,
        cost_estimate=pl.CostEstimate(
            flops=20 * rows * width, bytes_accessed=36 * rows * width, transcendentals=rows * width
        ),
        name="owner_update",
    )(tiles, master, one, two, average)


def place_kernel(where, *refs):
    pieces, out, sems = refs[:-2], refs[-2], refs[-1]
    copies = []
    for n, piece in enumerate(pieces):
        first = pl.multiple_of(where[n], SUB)
        copies.append(
            pltpu.make_async_copy(piece, out.at[pl.ds(first, piece.shape[0])], sems.at[n])
        )
    for copy in copies:
        copy.start()
    for copy in copies:
        copy.wait()


def place(where, pieces, rows):
    width = pieces[0].shape[1]
    return pl.pallas_call(
        place_kernel,
        in_specs=[pl.BlockSpec(memory_space=pltpu.SMEM)]
        + [pl.BlockSpec(memory_space=pltpu.VMEM)] * len(pieces),
        out_specs=pl.BlockSpec(memory_space=pl.ANY),
        out_shape=jax.ShapeDtypeStruct((rows, width), jnp.float32),
        scratch_shapes=[pltpu.SemaphoreType.DMA((len(pieces),))],
        cost_estimate=pl.CostEstimate(
            flops=0, bytes_accessed=8 * rows * width, transcendentals=0
        ),
        name="place",
    )(where, *pieces)


def arrange_kernel(at, *refs):
    groups, out = refs[:-1], refs[-1]
    for far in range(4):
        y = (at[1] + far) % 4
        for near in range(4):
            z = (at[0] + near) % 4
            cols = pl.ds(pl.multiple_of((z * 2 + y // 2) * LANES, LANES), LANES)
            for unit in range(groups[far].shape[1]):
                first = pl.multiple_of(unit * UNIT + y % 2 * SUB, SUB)
                out[pl.ds(first, SUB), cols] = groups[far][near, unit]


def arrange(at, groups):
    units = groups[0].shape[1]
    width = N_REP // 2 * LANES
    return pl.pallas_call(
        arrange_kernel,
        in_specs=[pl.BlockSpec(memory_space=pltpu.SMEM)]
        + [pl.BlockSpec(memory_space=pltpu.VMEM)] * 4,
        out_specs=pl.BlockSpec(memory_space=pltpu.VMEM),
        out_shape=jax.ShapeDtypeStruct((units * UNIT, width), jnp.float32),
        cost_estimate=pl.CostEstimate(
            flops=0, bytes_accessed=8 * units * UNIT * width, transcendentals=0
        ),
        name="arrange",
    )(at, *groups)


def pick_kernel(index, *refs):
    groups, out, window = refs[:4], refs[4], refs[5]
    units = groups[0].shape[1]
    for far in range(4):
        for core in range(2):
            for unit in range(units):
                window[(far * 2 + core) * units + unit] = groups[far][core, unit]
    for slot in range(out.shape[1]):
        at = index[slot]
        tile = window[jnp.maximum(at, 0)]
        tile = jnp.where(at >= 0, tile, jnp.zeros_like(tile))
        for copy in range(out.shape[0]):
            out[copy, slot] = tile


def pick(index, groups):
    units = groups[0].shape[1]
    slots = index.shape[0]
    return pl.pallas_call(
        pick_kernel,
        in_specs=[pl.BlockSpec(memory_space=pltpu.SMEM)]
        + [pl.BlockSpec(memory_space=pltpu.VMEM)] * 4,
        out_specs=pl.BlockSpec(memory_space=pltpu.VMEM),
        out_shape=jax.ShapeDtypeStruct((N_REP, slots, SUB, LANES), jnp.float32),
        scratch_shapes=[pltpu.VMEM((8 * units, SUB, LANES), jnp.float32)],
        cost_estimate=pl.CostEstimate(
            flops=0, bytes_accessed=4 * N_REP * slots * SUB * LANES, transcendentals=0
        ),
        name="pick",
    )(index, *groups)


def shift(array, axis, step):
    size = 2 if axis == "core" else 4
    return lax.ppermute(array, axis, [(i, (i + step) % size) for i in range(size)])


def gather_lines(lines):
    rows = lines.shape[0]
    half = rows // 2
    x, core = lax.axis_index("x"), lax.axis_index("core")
    left, right = shift(lines, "x", 1), shift(lines, "x", -1)
    upper, lower = shift(left[:half], "x", 1), shift(right[half:], "x", -1)
    pieces, where = [], []
    for piece, step, offset in (
        (lines, 0, 0),
        (left, 3, 0),
        (right, 1, 0),
        (upper, 2, 0),
        (lower, 2, half),
    ):
        chip = (x + step) % 4
        pieces += [piece, shift(piece, "core", 1)]
        where += [(chip * 2 + core) * rows + offset, (chip * 2 + 1 - core) * rows + offset]
    return place(jnp.stack(where).astype(jnp.int32), pieces, rows * N_SHARD)


def local(
    grads,
    master,
    moment_one,
    moment_two,
    average,
    tensor_owner,
    tensor_start,
    tensor_rows,
    tensor_slot,
):
    gradient = grads[0, 0]
    row_total, width = gradient.shape
    capacity = master.shape[1]
    blocks = width // LANES
    units = row_total // UNIT
    own_units = units // N_SHARD
    slots = capacity // UNIT
    rep = lax.axis_index(REP)
    shard = lax.axis_index(SHARD)
    col, half = rep // 2, rep % 2

    first = jnp.arange(units, dtype=jnp.int32) * UNIT
    inside = (first[:, None] >= tensor_start[None, :]) & (
        first[:, None] < (tensor_start + tensor_rows)[None, :]
    )
    home = tensor_owner * capacity + tensor_slot - tensor_start
    unit_home = jnp.sum(jnp.where(inside, home[None, :] + first[:, None], 0), axis=1) // UNIT
    slot_first = jnp.arange(slots, dtype=jnp.int32) * UNIT
    held = (
        (tensor_owner[None, :] == shard)
        & (slot_first[:, None] >= tensor_slot[None, :])
        & (slot_first[:, None] < (tensor_slot + tensor_rows)[None, :])
    )
    source = tensor_start - tensor_slot
    slot_unit = jnp.sum(jnp.where(held, source[None, :] + slot_first[:, None], 0), axis=1) // UNIT
    slot_used = jnp.any(held, axis=1)

    packed = gradient.reshape(N_SHARD, own_units, 2, SUB, blocks, LANES)
    packed = packed.transpose(4, 2, 0, 1, 3, 5).reshape(N_REP * N_SHARD, own_units, SUB, LANES)
    received = lax.all_to_all(packed, ALL, split_axis=0, concat_axis=0, tiled=True)
    summed = jnp.sum(received, axis=0, dtype=jnp.float32)

    def my_tiles(state):
        state = state.reshape(slots, 2, SUB, blocks, LANES)
        return lax.dynamic_slice(
            state, (0, half, 0, col, 0), (slots, 1, SUB, 1, LANES)
        ).reshape(slots, SUB, LANES)

    mine = jnp.stack([my_tiles(s[0]) for s in (master, moment_one, moment_two)], axis=1)
    sent = jnp.take(mine, unit_home % slots, axis=0)
    sent = jnp.where((unit_home // slots == shard)[:, None, None, None], sent, 0.0)
    sent = sent.reshape(N_SHARD, own_units, 3, SUB, LANES)
    sent = sent.reshape(4, 2, own_units, 3, SUB, LANES)
    x, core = lax.axis_index("x"), lax.axis_index("core")
    kept = lax.dynamic_index_in_dim(sent, core, axis=1, keepdims=False)
    given = lax.dynamic_index_in_dim(sent, 1 - core, axis=1, keepdims=False)
    merged = kept + shift(given, "core", 1)
    states = lax.dynamic_index_in_dim(merged, x, keepdims=False)
    for step in (1, 3, 2):
        piece = lax.dynamic_index_in_dim(merged, (x + step) % 4, keepdims=False)
        states = states + shift(piece, "x", step)

    weights, _, _ = new_master(summed, states[:, 0], states[:, 1], states[:, 2])
    z, y = lax.axis_index("z"), lax.axis_index("y")
    near = jnp.stack([weights] + [shift(weights, "z", step) for step in (3, 2, 1)])
    far = [near] + [shift(near, "y", step) for step in (3, 2, 1)]
    lines = arrange(jnp.stack([z, y]).astype(jnp.int32), far)
    new_params = gather_lines(lines)

    pair = jnp.stack([summed, shift(summed, "core", 1)])
    window = [pair] + [shift(pair, "x", step) for step in (3, 2, 1)]
    from_shard = slot_unit // own_units
    place_of = (from_shard // 2 - x + 4) % 4 * 2 + (from_shard + core) % 2
    index = place_of * own_units + slot_unit % own_units
    tiles = pick(jnp.where(slot_used, index, -1).astype(jnp.int32), window)
    tiles = lax.all_to_all(tiles, REP, split_axis=0, concat_axis=0, tiled=True)
    outs = owner_update(tiles, master[0], moment_one[0], moment_two[0], average[0])
    return (new_params, *(o[None] for o in outs))


def solution(mesh):
    grid = Mesh(mesh.devices.reshape(4, 4, 4, 2), ALL)
    state = P(SHARD, None, None)
    in_specs = (P(REP, SHARD, None, None), state, state, state, state, P(), P(), P(), P())
    out_specs = (P(), state, state, state, state)
    return jax.shard_map(local, mesh=grid, in_specs=in_specs, out_specs=out_specs, check_vma=False)
```

```python
import functools
import math

import jax
import jax.numpy as jnp
from jax import lax
from jax.experimental import pallas as pl
from jax.experimental.pallas import tpu as pltpu
from jax.sharding import Mesh, PartitionSpec as P

beta_one = 0.9
beta_two = 0.95
epsilon = 1e-08
learn_rate = 0.01
decay_base = 0.1
average_rate = 0.99
step_count = 10.0
reference_batch = 128.0

REP = ("z", "y")
SHARD = ("x", "core")
ALL = REP + SHARD
N_REP, N_SHARD = 16, 8
UNIT, SUB, LANES = 16, 8, 128
decay_scale = math.sqrt(N_REP * N_SHARD / reference_batch)


def new_master(summed, master, moment_one, moment_two):
    moment_one_new = beta_one * moment_one + (1.0 - beta_one) * summed
    moment_two_new = beta_two * moment_two + (1.0 - beta_two) * summed * summed
    moment = moment_one_new * (1.0 / (1.0 - beta_one**step_count))
    spread = jnp.sqrt(moment_two_new * (1.0 / (1.0 - beta_two**step_count)))
    update = moment / (spread + epsilon)
    master_new = master * (1.0 - learn_rate * decay_base * decay_scale) - learn_rate * update
    return master_new, moment_one_new, moment_two_new


def state_kernel(tiles, master, one, two, average, master_out, one_out, two_out, average_out):
    for unit in range(tiles.shape[1]):
        for half in range(2):
            rows = pl.ds(unit * UNIT + half * SUB, SUB)
            for block in range(N_REP // 2):
                cols = pl.ds(block * LANES, LANES)
                summed = tiles[block * 2 + half, unit]
                m, a, b = new_master(summed, master[rows, cols], one[rows, cols], two[rows, cols])
                master_out[rows, cols] = m
                one_out[rows, cols] = a
                two_out[rows, cols] = b
                average_out[rows, cols] = (
                    average_rate * average[rows, cols] + (1.0 - average_rate) * m
                )


def owner_update(tiles, master, one, two, average):
    rows, width = master.shape
    units = 8
    steps = rows // (units * UNIT)
    block = pl.BlockSpec((units * UNIT, width), lambda s: (s, 0))
    return pl.pallas_call(
        state_kernel,
        grid=(steps,),
        in_specs=[pl.BlockSpec((N_REP, units, SUB, LANES), lambda s: (0, s, 0, 0))] + [block] * 4,
        out_specs=[block] * 4,
        out_shape=[jax.ShapeDtypeStruct((rows, width), jnp.float32)] * 4,
        cost_estimate=pl.CostEstimate(
            flops=20 * rows * width, bytes_accessed=36 * rows * width, transcendentals=rows * width
        ),
        name="owner_update",
    )(tiles, master, one, two, average)


def place_kernel(count, where, *refs):
    pieces, out, sems = refs[:count], refs[-2], refs[-1]
    copies = []
    for n, piece in enumerate(pieces):
        first = pl.multiple_of(where[n], SUB)
        copies.append(
            pltpu.make_async_copy(piece, out.at[pl.ds(first, piece.shape[0])], sems.at[n])
        )
    for copy in copies:
        copy.start()
    for copy in copies:
        copy.wait()


def place(where, pieces, rows, held=None):
    width, count = pieces[0].shape[1], len(pieces)
    given = [] if held is None else [held]
    return pl.pallas_call(
        functools.partial(place_kernel, count),
        in_specs=[pl.BlockSpec(memory_space=pltpu.SMEM)]
        + [pl.BlockSpec(memory_space=pltpu.VMEM)] * count
        + [pl.BlockSpec(memory_space=pl.ANY)] * len(given),
        out_specs=pl.BlockSpec(memory_space=pl.ANY),
        out_shape=jax.ShapeDtypeStruct((rows, width), jnp.float32),
        scratch_shapes=[pltpu.SemaphoreType.DMA((count,))],
        input_output_aliases={} if held is None else {count + 1: 0},
        compiler_params=pltpu.CompilerParams(vmem_limit_bytes=6 << 20),
        cost_estimate=pl.CostEstimate(
            flops=0, bytes_accessed=8 * width * sum(p.shape[0] for p in pieces), transcendentals=0
        ),
        name="place",
    )(jnp.stack(where).astype(jnp.int32), *pieces, *given)


def arrange_kernel(at, *refs):
    groups, out = refs[:-1], refs[-1]
    for far in range(4):
        y = (at[1] + far) % 4
        for near in range(4):
            z = (at[0] + near) % 4
            cols = pl.ds(pl.multiple_of((z * 2 + y // 2) * LANES, LANES), LANES)
            for unit in range(groups[far].shape[1]):
                first = pl.multiple_of(unit * UNIT + y % 2 * SUB, SUB)
                out[pl.ds(first, SUB), cols] = groups[far][near, unit]


def arrange(at, groups):
    units = groups[0].shape[1]
    width = N_REP // 2 * LANES
    return pl.pallas_call(
        arrange_kernel,
        in_specs=[pl.BlockSpec(memory_space=pltpu.SMEM)]
        + [pl.BlockSpec(memory_space=pltpu.VMEM)] * 4,
        out_specs=pl.BlockSpec(memory_space=pltpu.VMEM),
        out_shape=jax.ShapeDtypeStruct((units * UNIT, width), jnp.float32),
        compiler_params=pltpu.CompilerParams(vmem_limit_bytes=4 << 20),
        cost_estimate=pl.CostEstimate(
            flops=0, bytes_accessed=8 * units * UNIT * width, transcendentals=0
        ),
        name="arrange",
    )(at, *groups)


def pick_kernel(index, *refs):
    groups, out, window = refs[:4], refs[4], refs[5]
    units = groups[0].shape[1]
    for far in range(4):
        for core in range(2):
            for unit in range(units):
                window[(far * 2 + core) * units + unit] = groups[far][core, unit]
    for slot in range(out.shape[1]):
        at = index[slot]
        tile = window[jnp.maximum(at, 0)]
        tile = jnp.where(at >= 0, tile, jnp.zeros_like(tile))
        for copy in range(out.shape[0]):
            out[copy, slot] = tile


def pick(index, groups):
    units = groups[0].shape[1]
    slots = index.shape[0]
    return pl.pallas_call(
        pick_kernel,
        in_specs=[pl.BlockSpec(memory_space=pltpu.SMEM)]
        + [pl.BlockSpec(memory_space=pltpu.VMEM)] * 4,
        out_specs=pl.BlockSpec(memory_space=pltpu.VMEM),
        out_shape=jax.ShapeDtypeStruct((N_REP, slots, SUB, LANES), jnp.float32),
        scratch_shapes=[pltpu.VMEM((8 * units, SUB, LANES), jnp.float32)],
        compiler_params=pltpu.CompilerParams(vmem_limit_bytes=4 << 20),
        cost_estimate=pl.CostEstimate(
            flops=0, bytes_accessed=4 * N_REP * slots * SUB * LANES, transcendentals=0
        ),
        name="pick",
    )(index, *groups)


def shift(array, axis, step):
    size = 2 if axis == "core" else 4
    return lax.ppermute(array, axis, [(i, (i + step) % size) for i in range(size)])


def gather_lines(lines):
    rows = lines.shape[0]
    half = rows // 2
    x, core = lax.axis_index("x"), lax.axis_index("core")
    left, right = shift(lines, "x", 1), shift(lines, "x", -1)
    upper, lower = shift(left[:half], "x", 1), shift(right[half:], "x", -1)
    out = None
    for group in (
        ((lines, 0, 0), (left, 3, 0), (right, 1, 0)),
        ((upper, 2, 0), (lower, 2, half)),
    ):
        pieces, where = [], []
        for piece, step, offset in group:
            chip = (x + step) % 4
            pieces += [piece, shift(piece, "core", 1)]
            where += [(chip * 2 + core) * rows + offset, (chip * 2 + 1 - core) * rows + offset]
        out = place(where, pieces, rows * N_SHARD, out)
    return out


def local(
    grads,
    master,
    moment_one,
    moment_two,
    average,
    tensor_owner,
    tensor_start,
    tensor_rows,
    tensor_slot,
):
    gradient = grads[0, 0]
    row_total, width = gradient.shape
    capacity = master.shape[1]
    blocks = width // LANES
    units = row_total // UNIT
    own_units = units // N_SHARD
    slots = capacity // UNIT
    rep = lax.axis_index(REP)
    shard = lax.axis_index(SHARD)
    col, half = rep // 2, rep % 2

    first = jnp.arange(units, dtype=jnp.int32) * UNIT
    inside = (first[:, None] >= tensor_start[None, :]) & (
        first[:, None] < (tensor_start + tensor_rows)[None, :]
    )
    home = tensor_owner * capacity + tensor_slot - tensor_start
    unit_home = jnp.sum(jnp.where(inside, home[None, :] + first[:, None], 0), axis=1) // UNIT
    slot_first = jnp.arange(slots, dtype=jnp.int32) * UNIT
    held = (
        (tensor_owner[None, :] == shard)
        & (slot_first[:, None] >= tensor_slot[None, :])
        & (slot_first[:, None] < (tensor_slot + tensor_rows)[None, :])
    )
    source = tensor_start - tensor_slot
    slot_unit = jnp.sum(jnp.where(held, source[None, :] + slot_first[:, None], 0), axis=1) // UNIT
    slot_used = jnp.any(held, axis=1)

    packed = gradient.reshape(N_SHARD, own_units, 2, SUB, blocks, LANES)
    packed = packed.transpose(4, 2, 0, 1, 3, 5).reshape(N_REP * N_SHARD, own_units, SUB, LANES)
    received = lax.all_to_all(packed, ALL, split_axis=0, concat_axis=0, tiled=True)
    summed = jnp.sum(received, axis=0, dtype=jnp.float32)

    def my_tiles(state):
        state = state.reshape(slots, 2, SUB, blocks, LANES)
        return lax.dynamic_slice(
            state, (0, half, 0, col, 0), (slots, 1, SUB, 1, LANES)
        ).reshape(slots, SUB, LANES)

    mine = jnp.stack([my_tiles(s[0]) for s in (master, moment_one, moment_two)], axis=1)
    sent = jnp.take(mine, unit_home % slots, axis=0)
    sent = jnp.where((unit_home // slots == shard)[:, None, None, None], sent, 0.0)
    sent = sent.reshape(N_SHARD, own_units, 3, SUB, LANES)
    sent = sent.reshape(4, 2, own_units, 3, SUB, LANES)
    x, core = lax.axis_index("x"), lax.axis_index("core")
    kept = lax.dynamic_index_in_dim(sent, core, axis=1, keepdims=False)
    given = lax.dynamic_index_in_dim(sent, 1 - core, axis=1, keepdims=False)
    merged = kept + shift(given, "core", 1)
    states = lax.dynamic_index_in_dim(merged, x, keepdims=False)
    for step in (1, 3, 2):
        piece = lax.dynamic_index_in_dim(merged, (x + step) % 4, keepdims=False)
        states = states + shift(piece, "x", step)

    weights, _, _ = new_master(summed, states[:, 0], states[:, 1], states[:, 2])
    z, y = lax.axis_index("z"), lax.axis_index("y")
    near = jnp.stack([weights] + [shift(weights, "z", step) for step in (3, 2, 1)])
    far = [near] + [shift(near, "y", step) for step in (3, 2, 1)]
    lines = arrange(jnp.stack([z, y]).astype(jnp.int32), far)
    new_params = gather_lines(lines)

    pair = jnp.stack([summed, shift(summed, "core", 1)])
    window = [pair] + [shift(pair, "x", step) for step in (3, 2, 1)]
    from_shard = slot_unit // own_units
    place_of = (from_shard // 2 - x + 4) % 4 * 2 + (from_shard + core) % 2
    index = place_of * own_units + slot_unit % own_units
    tiles = pick(jnp.where(slot_used, index, -1).astype(jnp.int32), window)
    tiles = lax.all_to_all(tiles, REP, split_axis=0, concat_axis=0, tiled=True)
    outs = owner_update(tiles, master[0], moment_one[0], moment_two[0], average[0])
    return (new_params, *(o[None] for o in outs))


def solution(mesh):
    grid = Mesh(mesh.devices.reshape(4, 4, 4, 2), ALL)
    state = P(SHARD, None, None)
    in_specs = (P(REP, SHARD, None, None), state, state, state, state, P(), P(), P(), P())
    out_specs = (P(), state, state, state, state)
    return jax.shard_map(local, mesh=grid, in_specs=in_specs, out_specs=out_specs, check_vma=False)
```

```python
import functools
import math

import jax
import jax.numpy as jnp
from jax import lax
from jax.experimental import pallas as pl
from jax.experimental.pallas import tpu as pltpu
from jax.sharding import Mesh, PartitionSpec as P

beta_one = 0.9
beta_two = 0.95
epsilon = 1e-08
learn_rate = 0.01
decay_base = 0.1
average_rate = 0.99
step_count = 10.0
reference_batch = 128.0

REP = ("z", "y")
SHARD = ("x", "core")
ALL = REP + SHARD
N_REP, N_SHARD = 16, 8
UNIT, SUB, LANES = 16, 8, 128
decay_scale = math.sqrt(N_REP * N_SHARD / reference_batch)


def new_master(summed, master, moment_one, moment_two):
    moment_one_new = beta_one * moment_one + (1.0 - beta_one) * summed
    moment_two_new = beta_two * moment_two + (1.0 - beta_two) * summed * summed
    moment = moment_one_new * (1.0 / (1.0 - beta_one**step_count))
    spread = jnp.sqrt(moment_two_new * (1.0 / (1.0 - beta_two**step_count)))
    update = moment / (spread + epsilon)
    master_new = master * (1.0 - learn_rate * decay_base * decay_scale) - learn_rate * update
    return master_new, moment_one_new, moment_two_new


def state_kernel(tiles, master, one, two, average, master_out, one_out, two_out, average_out):
    for unit in range(tiles.shape[1]):
        for half in range(2):
            rows = pl.ds(unit * UNIT + half * SUB, SUB)
            for block in range(N_REP // 2):
                cols = pl.ds(block * LANES, LANES)
                summed = tiles[block * 2 + half, unit]
                m, a, b = new_master(summed, master[rows, cols], one[rows, cols], two[rows, cols])
                master_out[rows, cols] = m
                one_out[rows, cols] = a
                two_out[rows, cols] = b
                average_out[rows, cols] = (
                    average_rate * average[rows, cols] + (1.0 - average_rate) * m
                )


def owner_update(tiles, master, one, two, average):
    rows, width = master.shape
    units = 8
    steps = rows // (units * UNIT)
    block = pl.BlockSpec((units * UNIT, width), lambda s: (s, 0))
    return pl.pallas_call(
        state_kernel,
        grid=(steps,),
        in_specs=[pl.BlockSpec((N_REP, units, SUB, LANES), lambda s: (0, s, 0, 0))] + [block] * 4,
        out_specs=[block] * 4,
        out_shape=[jax.ShapeDtypeStruct((rows, width), jnp.float32)] * 4,
        cost_estimate=pl.CostEstimate(
            flops=20 * rows * width, bytes_accessed=36 * rows * width, transcendentals=rows * width
        ),
        name="owner_update",
    )(tiles, master, one, two, average)


def place_kernel(count, where, *refs):
    pieces, out, sems = refs[:count], refs[-2], refs[-1]
    copies = []
    for n, piece in enumerate(pieces):
        first = pl.multiple_of(where[n], SUB)
        copies.append(
            pltpu.make_async_copy(piece, out.at[pl.ds(first, piece.shape[0])], sems.at[n])
        )
    for copy in copies:
        copy.start()
    for copy in copies:
        copy.wait()


def place(where, pieces, rows, held=None):
    width, count = pieces[0].shape[1], len(pieces)
    given = [] if held is None else [held]
    return pl.pallas_call(
        functools.partial(place_kernel, count),
        in_specs=[pl.BlockSpec(memory_space=pltpu.SMEM)]
        + [pl.BlockSpec(memory_space=pltpu.VMEM)] * count
        + [pl.BlockSpec(memory_space=pl.ANY)] * len(given),
        out_specs=pl.BlockSpec(memory_space=pl.ANY),
        out_shape=jax.ShapeDtypeStruct((rows, width), jnp.float32),
        scratch_shapes=[pltpu.SemaphoreType.DMA((count,))],
        input_output_aliases={} if held is None else {count + 1: 0},
        compiler_params=pltpu.CompilerParams(vmem_limit_bytes=6 << 20),
        cost_estimate=pl.CostEstimate(
            flops=0, bytes_accessed=8 * width * sum(p.shape[0] for p in pieces), transcendentals=0
        ),
        name="place",
    )(jnp.stack(where).astype(jnp.int32), *pieces, *given)


def arrange_kernel(at, *refs):
    groups, out = refs[:-1], refs[-1]
    for far in range(4):
        y = (at[1] + far) % 4
        for near in range(4):
            z = (at[0] + near) % 4
            cols = pl.ds(pl.multiple_of((z * 2 + y // 2) * LANES, LANES), LANES)
            for unit in range(groups[far].shape[1]):
                first = pl.multiple_of(unit * UNIT + y % 2 * SUB, SUB)
                out[pl.ds(first, SUB), cols] = groups[far][near, unit]


def arrange(at, groups):
    units = groups[0].shape[1]
    width = N_REP // 2 * LANES
    return pl.pallas_call(
        arrange_kernel,
        in_specs=[pl.BlockSpec(memory_space=pltpu.SMEM)]
        + [pl.BlockSpec(memory_space=pltpu.VMEM)] * 4,
        out_specs=pl.BlockSpec(memory_space=pltpu.VMEM),
        out_shape=jax.ShapeDtypeStruct((units * UNIT, width), jnp.float32),
        compiler_params=pltpu.CompilerParams(vmem_limit_bytes=4 << 20),
        cost_estimate=pl.CostEstimate(
            flops=0, bytes_accessed=8 * units * UNIT * width, transcendentals=0
        ),
        name="arrange",
    )(at, *groups)


def pick_kernel(index, same, other, out, window):
    near, units = same.shape[:2]
    for step in range(near):
        for unit in range(units):
            window[step * units + unit] = same[step, unit]
            window[(near + step) * units + unit] = other[step, unit]
    for slot in range(out.shape[1]):
        at = index[slot]
        tile = window[jnp.maximum(at, 0)]
        tile = jnp.where(at >= 0, tile, jnp.zeros_like(tile))
        for copy in range(out.shape[0]):
            out[copy, slot] = tile


def pick(index, same, other):
    slots, units = index.shape[0], same.shape[0] * same.shape[1]
    return pl.pallas_call(
        pick_kernel,
        in_specs=[pl.BlockSpec(memory_space=pltpu.SMEM)]
        + [pl.BlockSpec(memory_space=pltpu.VMEM)] * 2,
        out_specs=pl.BlockSpec(memory_space=pltpu.VMEM),
        out_shape=jax.ShapeDtypeStruct((N_REP, slots, SUB, LANES), jnp.float32),
        scratch_shapes=[pltpu.VMEM((2 * units, SUB, LANES), jnp.float32)],
        compiler_params=pltpu.CompilerParams(vmem_limit_bytes=4 << 20),
        cost_estimate=pl.CostEstimate(
            flops=0, bytes_accessed=4 * N_REP * slots * SUB * LANES, transcendentals=0
        ),
        name="pick",
    )(index, same, other)


def tile_kernel(given, out, held, sems):
    steps = held.shape[0]
    units = held.shape[1]
    loads = [
        pltpu.make_async_copy(given.at[pl.ds(step * units, units)], held.at[step], sems.at[step])
        for step in range(steps)
    ]
    for load in loads:
        load.start()
    for step in range(steps):
        loads[step].wait()
        for block in range(out.shape[0] // 2):
            lanes = pl.ds(block * LANES, LANES)
            for half in range(2):
                out[block * 2 + half, pl.ds(step * units, units)] = held[step, :, half, :, lanes]


def tile_order(gradient):
    rows, width = gradient.shape
    units = rows // UNIT
    return pl.pallas_call(
        tile_kernel,
        in_specs=[pl.BlockSpec(memory_space=pl.ANY)],
        out_specs=pl.BlockSpec(memory_space=pltpu.VMEM),
        out_shape=jax.ShapeDtypeStruct((N_REP, units, SUB, LANES), gradient.dtype),
        scratch_shapes=[
            pltpu.VMEM((8, units // 8, 2, SUB, width), gradient.dtype),
            pltpu.SemaphoreType.DMA((8,)),
        ],
        cost_estimate=pl.CostEstimate(
            flops=0, bytes_accessed=4 * rows * width, transcendentals=0
        ),
        name="tile_order",
    )(gradient.reshape(units, 2, SUB, width))


def shift(array, axis, step):
    size = 2 if axis == "core" else 4
    return lax.ppermute(array, axis, [(i, (i + step) % size) for i in range(size)])


def gather_lines(lines):
    rows = lines.shape[0]
    half = rows // 2
    x, core = lax.axis_index("x"), lax.axis_index("core")
    left, right = shift(lines, "x", 1), shift(lines, "x", -1)
    upper, lower = shift(left[:half], "x", 1), shift(right[half:], "x", -1)
    out = None
    for group in (
        ((lines, 0, 0), (left, 3, 0), (right, 1, 0)),
        ((upper, 2, 0), (lower, 2, half)),
    ):
        pieces, where = [], []
        for piece, step, offset in group:
            chip = (x + step) % 4
            pieces += [piece, shift(piece, "core", 1)]
            where += [(chip * 2 + core) * rows + offset, (chip * 2 + 1 - core) * rows + offset]
        out = place(where, pieces, rows * N_SHARD, out)
    return out


def local(
    grads,
    master,
    moment_one,
    moment_two,
    average,
    tensor_owner,
    tensor_start,
    tensor_rows,
    tensor_slot,
):
    gradient = grads[0, 0]
    row_total, width = gradient.shape
    capacity = master.shape[1]
    blocks = width // LANES
    units = row_total // UNIT
    own_units = units // N_SHARD
    slots = capacity // UNIT
    rep = lax.axis_index(REP)
    shard = lax.axis_index(SHARD)
    col, half = rep // 2, rep % 2

    first = jnp.arange(units, dtype=jnp.int32) * UNIT
    inside = (first[:, None] >= tensor_start[None, :]) & (
        first[:, None] < (tensor_start + tensor_rows)[None, :]
    )
    home = tensor_owner * capacity + tensor_slot - tensor_start
    unit_home = jnp.sum(jnp.where(inside, home[None, :] + first[:, None], 0), axis=1) // UNIT
    slot_first = jnp.arange(slots, dtype=jnp.int32) * UNIT
    held = (
        (tensor_owner[None, :] == shard)
        & (slot_first[:, None] >= tensor_slot[None, :])
        & (slot_first[:, None] < (tensor_slot + tensor_rows)[None, :])
    )
    source = tensor_start - tensor_slot
    slot_unit = jnp.sum(jnp.where(held, source[None, :] + slot_first[:, None], 0), axis=1) // UNIT
    slot_used = jnp.any(held, axis=1)

    packed = tile_order(gradient).reshape(N_REP * N_SHARD, own_units, SUB, LANES)
    received = lax.all_to_all(packed, ALL, split_axis=0, concat_axis=0, tiled=True)
    summed = jnp.sum(received, axis=0, dtype=jnp.float32)

    def my_tiles(state):
        state = state.reshape(slots, 2, SUB, blocks, LANES)
        return lax.dynamic_slice(
            state, (0, half, 0, col, 0), (slots, 1, SUB, 1, LANES)
        ).reshape(slots, SUB, LANES)

    mine = jnp.stack([my_tiles(s[0]) for s in (master, moment_one, moment_two)], axis=1)
    sent = jnp.take(mine, unit_home % slots, axis=0)
    sent = jnp.where((unit_home // slots == shard)[:, None, None, None], sent, 0.0)
    sent = sent.reshape(N_SHARD, own_units, 3, SUB, LANES)
    sent = sent.reshape(4, 2, own_units, 3, SUB, LANES)
    x, core = lax.axis_index("x"), lax.axis_index("core")
    kept = lax.dynamic_index_in_dim(sent, core, axis=1, keepdims=False)
    given = lax.dynamic_index_in_dim(sent, 1 - core, axis=1, keepdims=False)
    merged = kept + shift(given, "core", 1)
    states = lax.dynamic_index_in_dim(merged, x, keepdims=False)
    for step in (1, 3, 2):
        piece = lax.dynamic_index_in_dim(merged, (x + step) % 4, keepdims=False)
        states = states + shift(piece, "x", step)

    weights, _, _ = new_master(summed, states[:, 0], states[:, 1], states[:, 2])
    z, y = lax.axis_index("z"), lax.axis_index("y")
    near = jnp.stack([weights] + [shift(weights, "z", step) for step in (3, 2, 1)])
    far = [near] + [shift(near, "y", step) for step in (3, 2, 1)]
    lines = arrange(jnp.stack([z, y]).astype(jnp.int32), far)
    new_params = gather_lines(lines)

    same = jnp.stack([summed] + [shift(summed, "x", step) for step in (3, 2, 1)])
    other = shift(same, "core", 1)
    from_shard = slot_unit // own_units
    index = (from_shard + core) % 2 * 4 + (from_shard // 2 - x + 4) % 4
    index = index * own_units + slot_unit % own_units
    tiles = pick(jnp.where(slot_used, index, -1).astype(jnp.int32), same, other)
    tiles = lax.all_to_all(tiles, REP, split_axis=0, concat_axis=0, tiled=True)
    outs = owner_update(tiles, master[0], moment_one[0], moment_two[0], average[0])
    return (new_params, *(o[None] for o in outs))


def solution(mesh):
    grid = Mesh(mesh.devices.reshape(4, 4, 4, 2), ALL)
    state = P(SHARD, None, None)
    in_specs = (P(REP, SHARD, None, None), state, state, state, state, P(), P(), P(), P())
    out_specs = (P(), state, state, state, state)
    return jax.shard_map(local, mesh=grid, in_specs=in_specs, out_specs=out_specs, check_vma=False)
```

```python
import functools
import math

import jax
import jax.numpy as jnp
from jax import lax
from jax.experimental import pallas as pl
from jax.experimental.pallas import tpu as pltpu
from jax.sharding import Mesh, PartitionSpec as P

beta_one = 0.9
beta_two = 0.95
epsilon = 1e-08
learn_rate = 0.01
decay_base = 0.1
average_rate = 0.99
step_count = 10.0
reference_batch = 128.0

REP = ("z", "y")
SHARD = ("x", "core")
ALL = REP + SHARD
N_REP, N_SHARD = 16, 8
UNIT, SUB, LANES = 16, 8, 128
decay_scale = math.sqrt(N_REP * N_SHARD / reference_batch)


def new_master(summed, master, moment_one, moment_two):
    moment_one_new = beta_one * moment_one + (1.0 - beta_one) * summed
    moment_two_new = beta_two * moment_two + (1.0 - beta_two) * summed * summed
    moment = moment_one_new * (1.0 / (1.0 - beta_one**step_count))
    spread = jnp.sqrt(moment_two_new * (1.0 / (1.0 - beta_two**step_count)))
    update = moment / (spread + epsilon)
    master_new = master * (1.0 - learn_rate * decay_base * decay_scale) - learn_rate * update
    return master_new, moment_one_new, moment_two_new


def state_kernel(where, tiles, master, one, two, average, *refs):
    pieces, (master_out, one_out, two_out, average_out, out, sems) = refs[:4], refs[5:]
    copies = []
    for n, piece in enumerate(pieces):
        first = pl.multiple_of(where[n], SUB)
        copies.append(
            pltpu.make_async_copy(piece, out.at[pl.ds(first, piece.shape[0])], sems.at[n])
        )

    @pl.when(pl.program_id(0) == 0)
    def _():
        for copy in copies:
            copy.start()

    for unit in range(tiles.shape[1]):
        for half in range(2):
            rows = pl.ds(unit * UNIT + half * SUB, SUB)
            for block in range(N_REP // 2):
                cols = pl.ds(block * LANES, LANES)
                summed = tiles[block * 2 + half, unit]
                m, a, b = new_master(summed, master[rows, cols], one[rows, cols], two[rows, cols])
                master_out[rows, cols] = m
                one_out[rows, cols] = a
                two_out[rows, cols] = b
                average_out[rows, cols] = (
                    average_rate * average[rows, cols] + (1.0 - average_rate) * m
                )

    @pl.when(pl.program_id(0) == pl.num_programs(0) - 1)
    def _():
        for copy in copies:
            copy.wait()


def owner_update(tiles, master, one, two, average, where, pieces, held):
    rows, width = master.shape
    units = 8
    steps = rows // (units * UNIT)
    block = pl.BlockSpec((units * UNIT, width), lambda s: (s, 0))
    return pl.pallas_call(
        state_kernel,
        grid=(steps,),
        in_specs=[
            pl.BlockSpec(memory_space=pltpu.SMEM),
            pl.BlockSpec((N_REP, units, SUB, LANES), lambda s: (0, s, 0, 0)),
        ]
        + [block] * 4
        + [pl.BlockSpec(piece.shape, lambda s: (0, 0)) for piece in pieces]
        + [pl.BlockSpec(memory_space=pl.ANY)],
        out_specs=[block] * 4 + [pl.BlockSpec(memory_space=pl.ANY)],
        out_shape=[jax.ShapeDtypeStruct((rows, width), jnp.float32)] * 4
        + [jax.ShapeDtypeStruct(held.shape, jnp.float32)],
        scratch_shapes=[pltpu.SemaphoreType.DMA((4,))],
        input_output_aliases={10: 4},
        cost_estimate=pl.CostEstimate(
            flops=20 * rows * width, bytes_accessed=36 * rows * width, transcendentals=rows * width
        ),
        name="owner_update",
    )(where, tiles, master, one, two, average, *pieces, held)


def place_kernel(count, where, *refs):
    pieces, out, sems = refs[:count], refs[-2], refs[-1]
    copies = []
    for n, piece in enumerate(pieces):
        first = pl.multiple_of(where[n], SUB)
        copies.append(
            pltpu.make_async_copy(piece, out.at[pl.ds(first, piece.shape[0])], sems.at[n])
        )
    for copy in copies:
        copy.start()
    for copy in copies:
        copy.wait()


def place(where, pieces, rows, held=None):
    width, count = pieces[0].shape[1], len(pieces)
    given = [] if held is None else [held]
    return pl.pallas_call(
        functools.partial(place_kernel, count),
        in_specs=[pl.BlockSpec(memory_space=pltpu.SMEM)]
        + [pl.BlockSpec(memory_space=pltpu.VMEM)] * count
        + [pl.BlockSpec(memory_space=pl.ANY)] * len(given),
        out_specs=pl.BlockSpec(memory_space=pl.ANY),
        out_shape=jax.ShapeDtypeStruct((rows, width), jnp.float32),
        scratch_shapes=[pltpu.SemaphoreType.DMA((count,))],
        input_output_aliases={} if held is None else {count + 1: 0},
        compiler_params=pltpu.CompilerParams(vmem_limit_bytes=6 << 20),
        cost_estimate=pl.CostEstimate(
            flops=0, bytes_accessed=8 * width * sum(p.shape[0] for p in pieces), transcendentals=0
        ),
        name="place",
    )(jnp.stack(where).astype(jnp.int32), *pieces, *given)


def arrange_kernel(at, *refs):
    groups, out = refs[:-1], refs[-1]
    for far in range(4):
        y = (at[1] + far) % 4
        for near in range(4):
            z = (at[0] + near) % 4
            cols = pl.ds(pl.multiple_of((z * 2 + y // 2) * LANES, LANES), LANES)
            for unit in range(groups[far].shape[1]):
                first = pl.multiple_of(unit * UNIT + y % 2 * SUB, SUB)
                out[pl.ds(first, SUB), cols] = groups[far][near, unit]


def arrange(at, groups):
    units = groups[0].shape[1]
    width = N_REP // 2 * LANES
    return pl.pallas_call(
        arrange_kernel,
        in_specs=[pl.BlockSpec(memory_space=pltpu.SMEM)]
        + [pl.BlockSpec(memory_space=pltpu.VMEM)] * 4,
        out_specs=pl.BlockSpec(memory_space=pltpu.VMEM),
        out_shape=jax.ShapeDtypeStruct((units * UNIT, width), jnp.float32),
        compiler_params=pltpu.CompilerParams(vmem_limit_bytes=4 << 20),
        cost_estimate=pl.CostEstimate(
            flops=0, bytes_accessed=8 * units * UNIT * width, transcendentals=0
        ),
        name="arrange",
    )(at, *groups)


def pick_kernel(index, same, other, out, window):
    near, units = same.shape[:2]
    for step in range(near):
        for unit in range(units):
            window[step * units + unit] = same[step, unit]
            window[(near + step) * units + unit] = other[step, unit]
    for slot in range(out.shape[1]):
        at = index[slot]
        tile = window[jnp.maximum(at, 0)]
        tile = jnp.where(at >= 0, tile, jnp.zeros_like(tile))
        for copy in range(out.shape[0]):
            out[copy, slot] = tile


def pick(index, same, other):
    slots, units = index.shape[0], same.shape[0] * same.shape[1]
    return pl.pallas_call(
        pick_kernel,
        in_specs=[pl.BlockSpec(memory_space=pltpu.SMEM)]
        + [pl.BlockSpec(memory_space=pltpu.VMEM)] * 2,
        out_specs=pl.BlockSpec(memory_space=pltpu.VMEM),
        out_shape=jax.ShapeDtypeStruct((N_REP, slots, SUB, LANES), jnp.float32),
        scratch_shapes=[pltpu.VMEM((2 * units, SUB, LANES), jnp.float32)],
        compiler_params=pltpu.CompilerParams(vmem_limit_bytes=4 << 20),
        cost_estimate=pl.CostEstimate(
            flops=0, bytes_accessed=4 * N_REP * slots * SUB * LANES, transcendentals=0
        ),
        name="pick",
    )(index, same, other)


def tile_kernel(given, out, held, sems):
    steps = held.shape[0]
    units = held.shape[1]
    loads = [
        pltpu.make_async_copy(given.at[pl.ds(step * units, units)], held.at[step], sems.at[step])
        for step in range(steps)
    ]
    for load in loads:
        load.start()
    for step in range(steps):
        loads[step].wait()
        for block in range(out.shape[0] // 2):
            lanes = pl.ds(block * LANES, LANES)
            for half in range(2):
                out[block * 2 + half, pl.ds(step * units, units)] = held[step, :, half, :, lanes]


def tile_order(gradient):
    rows, width = gradient.shape
    units = rows // UNIT
    return pl.pallas_call(
        tile_kernel,
        in_specs=[pl.BlockSpec(memory_space=pl.ANY)],
        out_specs=pl.BlockSpec(memory_space=pltpu.VMEM),
        out_shape=jax.ShapeDtypeStruct((N_REP, units, SUB, LANES), gradient.dtype),
        scratch_shapes=[
            pltpu.VMEM((8, units // 8, 2, SUB, width), gradient.dtype),
            pltpu.SemaphoreType.DMA((8,)),
        ],
        cost_estimate=pl.CostEstimate(
            flops=0, bytes_accessed=4 * rows * width, transcendentals=0
        ),
        name="tile_order",
    )(gradient.reshape(units, 2, SUB, width))


def shift(array, axis, step):
    size = 2 if axis == "core" else 4
    return lax.ppermute(array, axis, [(i, (i + step) % size) for i in range(size)])


def gather_lines(lines):
    rows = lines.shape[0]
    half = rows // 2
    x, core = lax.axis_index("x"), lax.axis_index("core")
    left, right = shift(lines, "x", 1), shift(lines, "x", -1)
    upper, lower = shift(left[:half], "x", 1), shift(right[half:], "x", -1)
    out = None
    for group in (
        ((lines, 0, 0), (left, 3, 0), (right, 1, 0)),
        ((upper, 2, 0), (lower, 2, half)),
    ):
        pieces, where = [], []
        for piece, step, offset in group:
            chip = (x + step) % 4
            pieces += [piece, shift(piece, "core", 1)]
            where += [(chip * 2 + core) * rows + offset, (chip * 2 + 1 - core) * rows + offset]
        if out is None:
            out = place(where, pieces, rows * N_SHARD)
    return jnp.stack(where).astype(jnp.int32), pieces, out


def local(
    grads,
    master,
    moment_one,
    moment_two,
    average,
    tensor_owner,
    tensor_start,
    tensor_rows,
    tensor_slot,
):
    gradient = grads[0, 0]
    row_total, width = gradient.shape
    capacity = master.shape[1]
    blocks = width // LANES
    units = row_total // UNIT
    own_units = units // N_SHARD
    slots = capacity // UNIT
    rep = lax.axis_index(REP)
    shard = lax.axis_index(SHARD)
    col, half = rep // 2, rep % 2

    first = jnp.arange(units, dtype=jnp.int32) * UNIT
    inside = (first[:, None] >= tensor_start[None, :]) & (
        first[:, None] < (tensor_start + tensor_rows)[None, :]
    )
    home = tensor_owner * capacity + tensor_slot - tensor_start
    unit_home = jnp.sum(jnp.where(inside, home[None, :] + first[:, None], 0), axis=1) // UNIT
    slot_first = jnp.arange(slots, dtype=jnp.int32) * UNIT
    held = (
        (tensor_owner[None, :] == shard)
        & (slot_first[:, None] >= tensor_slot[None, :])
        & (slot_first[:, None] < (tensor_slot + tensor_rows)[None, :])
    )
    source = tensor_start - tensor_slot
    slot_unit = jnp.sum(jnp.where(held, source[None, :] + slot_first[:, None], 0), axis=1) // UNIT
    slot_used = jnp.any(held, axis=1)

    packed = tile_order(gradient).reshape(N_REP * N_SHARD, own_units, SUB, LANES)
    received = lax.all_to_all(packed, ALL, split_axis=0, concat_axis=0, tiled=True)
    summed = jnp.sum(received, axis=0, dtype=jnp.float32)

    def my_tiles(state):
        state = state.reshape(slots, 2, SUB, blocks, LANES)
        return lax.dynamic_slice(
            state, (0, half, 0, col, 0), (slots, 1, SUB, 1, LANES)
        ).reshape(slots, SUB, LANES)

    mine = jnp.stack([my_tiles(s[0]) for s in (master, moment_one, moment_two)], axis=1)
    sent = jnp.take(mine, unit_home % slots, axis=0)
    sent = jnp.where((unit_home // slots == shard)[:, None, None, None], sent, 0.0)
    sent = sent.reshape(N_SHARD, own_units, 3, SUB, LANES)
    sent = sent.reshape(4, 2, own_units, 3, SUB, LANES)
    x, core = lax.axis_index("x"), lax.axis_index("core")
    kept = lax.dynamic_index_in_dim(sent, core, axis=1, keepdims=False)
    given = lax.dynamic_index_in_dim(sent, 1 - core, axis=1, keepdims=False)
    merged = kept + shift(given, "core", 1)
    states = lax.dynamic_index_in_dim(merged, x, keepdims=False)
    for step in (1, 3, 2):
        piece = lax.dynamic_index_in_dim(merged, (x + step) % 4, keepdims=False)
        states = states + shift(piece, "x", step)

    weights, _, _ = new_master(summed, states[:, 0], states[:, 1], states[:, 2])
    z, y = lax.axis_index("z"), lax.axis_index("y")
    near = jnp.stack([weights] + [shift(weights, "z", step) for step in (3, 2, 1)])
    far = [near] + [shift(near, "y", step) for step in (3, 2, 1)]
    lines = arrange(jnp.stack([z, y]).astype(jnp.int32), far)
    where, pieces, window = gather_lines(lines)

    same = jnp.stack([summed] + [shift(summed, "x", step) for step in (3, 2, 1)])
    other = shift(same, "core", 1)
    from_shard = slot_unit // own_units
    index = (from_shard + core) % 2 * 4 + (from_shard // 2 - x + 4) % 4
    index = index * own_units + slot_unit % own_units
    tiles = pick(jnp.where(slot_used, index, -1).astype(jnp.int32), same, other)
    tiles = lax.all_to_all(tiles, REP, split_axis=0, concat_axis=0, tiled=True)
    *outs, new_params = owner_update(
        tiles, master[0], moment_one[0], moment_two[0], average[0], where, pieces, window
    )
    return (new_params, *(o[None] for o in outs))


def solution(mesh):
    grid = Mesh(mesh.devices.reshape(4, 4, 4, 2), ALL)
    state = P(SHARD, None, None)
    in_specs = (P(REP, SHARD, None, None), state, state, state, state, P(), P(), P(), P())
    out_specs = (P(), state, state, state, state)
    return jax.shard_map(local, mesh=grid, in_specs=in_specs, out_specs=out_specs, check_vma=False)
```
